128 devices in a mesh: rep: 16 (over x, y), shard: 8 (over z, core).
Axes of the slice: x: 4, y: 4, z: 4, core: 2. Of those that a mesh axis runs over, the one named last changes fastest.
Arguments:
- sq_grad: float32 [96, 768, 768], P(None, ('rep', 'shard'))
- sq_moment: float32 [96, 768, 768], P(None, ('rep', 'shard')), may hold values from -6 to 6
- sq_weight: float32 [96, 768, 768], P(None, ('rep', 'shard')), may hold values from -0.21875 to 0.21875
- in_grad: float32 [16, 768, 3072], P(None, ('rep', 'shard'))
- in_moment: float32 [16, 768, 3072], P(None, ('rep', 'shard')), may hold values from -6 to 6
- in_weight: float32 [16, 768, 3072], P(None, ('rep', 'shard')), may hold values from -0.21875 to 0.21875
- out_grad: float32 [16, 3072, 768], P(None, ('rep', 'shard'))
- out_moment: float32 [16, 3072, 768], P(None, ('rep', 'shard')), may hold values from -6 to 6
- out_weight: float32 [16, 3072, 768], P(None, ('rep', 'shard')), may hold values from -0.109375 to 0.109375
- emb_grad: float32 [3072, 768], P(('rep', 'shard'))
- emb_moment: float32 [3072, 768], P(('rep', 'shard')), may hold values from -6 to 6
- emb_weight: float32 [3072, 768], P(('rep', 'shard')), may hold values from -0.21875 to 0.21875
Outputs:
- sq_moment_new: float32 [96, 768, 768], P(None, ('rep', 'shard'))
- sq_weight_new: float32 [96, 768, 768], P(None, ('rep', 'shard'))
- sq_direction: float32 [96, 768, 768], P(None, ('rep', 'shard'))
- in_moment_new: float32 [16, 768, 3072], P(None, ('rep', 'shard'))
- in_weight_new: float32 [16, 768, 3072], P(None, ('rep', 'shard'))
- in_direction: float32 [16, 768, 3072], P(None, ('rep', 'shard'))
- out_moment_new: float32 [16, 3072, 768], P(None, ('rep', 'shard'))
- out_weight_new: float32 [16, 3072, 768], P(None, ('rep', 'shard'))
- out_direction: float32 [16, 3072, 768], P(None, ('rep', 'shard'))
- emb_moment_new: float32 [3072, 768], P(('rep', 'shard'))
- emb_weight_new: float32 [3072, 768], P(('rep', 'shard'))
- emb_direction: float32 [3072, 768], P(('rep', 'shard'))
The draws below stay inside these ranges and needn't reach their ends.
All inputs are finite; a program needn't handle non-finite values.
Results may differ from the reference program's by a relative error of at most 0.019.
Values may be sent and summed in bfloat16 or wider, within the bound.
No kernel may reach another device: no remote copies, remote signals or barrier semaphores. Data moves between devices by JAX's collectives and lax.ppermute only.
A program may use at most 192 MiB of HBM per device.

```python
import math
import jax
import jax.numpy as jnp
from jax import lax

D = 768
FF = 3072
V = 3072
ITERS = 3
NSQ = 96
NIN = 16
NOUT = 16


def rough_field(key, shape):
    first_key, second_key, third_key = jax.random.split(key, 3)
    leading = shape[:-2]
    row_count = shape[-2]
    col_count = shape[-1]
    top_log = math.log(10.0)
    row_scale = jnp.exp(jax.random.uniform(first_key, leading + (row_count, 1), jnp.float32, 0.0, top_log))
    col_scale = jnp.exp(jax.random.uniform(second_key, leading + (1, col_count), jnp.float32, 0.0, top_log))
    base = jax.random.normal(third_key, shape, jnp.float32)
    return base * row_scale * col_scale / 10.0


def draw_sq_grad(key, part):
    return rough_field(jax.random.fold_in(key, 11), (NSQ, D, D))


def draw_in_grad(key, part):
    return rough_field(jax.random.fold_in(key, 12), (NIN, D, FF))


def draw_out_grad(key, part):
    return rough_field(jax.random.fold_in(key, 13), (NOUT, FF, D))


def draw_emb_grad(key, part):
    return rough_field(jax.random.fold_in(key, 14), (V, D))


def shard_levels(key, shape, pieces, smallest, largest):
    gain, own = 1.0, jax.random.fold_in(key, 6)
    for dim, parts in pieces:
        steps = jnp.exp(jax.random.uniform(jax.random.fold_in(own, dim), (parts,), jnp.float32, smallest / len(pieces), largest / len(pieces)))
        gain = gain * jnp.repeat(steps, shape[dim] // parts).reshape([-1 if axis == dim else 1 for axis in range(len(shape))])
    return gain


def scatter_about(rng, dims, scale, most, cuts=(), kind=jnp.bfloat16):
    loudness = shard_levels(rng, dims, cuts, -0.22, 0.18) if cuts else 1.0
    drawn = jax.random.normal(rng, dims, jnp.float32) * scale * loudness
    return jnp.minimum(jnp.maximum(drawn, -most), most).astype(kind)


def setup_inputs(seed: int = 0) -> dict:
    key_of = jax.random.split(jax.random.key(seed), 13)
    sq_grad = draw_sq_grad(jax.random.fold_in(key_of[12], 71), 0)
    sq_moment = scatter_about(key_of[1], (NSQ, D, D), 1.0, 6.0, ((1, 128),), jnp.float32)
    sq_weight = scatter_about(key_of[2], (NSQ, D, D), D ** -0.5, 0.21875, ((1, 128),), jnp.float32)
    in_grad = draw_in_grad(jax.random.fold_in(key_of[12], 71), 0)
    in_moment = scatter_about(key_of[4], (NIN, D, FF), 1.0, 6.0, ((1, 128),), jnp.float32)
    in_weight = scatter_about(key_of[5], (NIN, D, FF), D ** -0.5, 0.21875, ((1, 128),), jnp.float32)
    out_grad = draw_out_grad(jax.random.fold_in(key_of[12], 71), 0)
    out_moment = scatter_about(key_of[7], (NOUT, FF, D), 1.0, 6.0, ((1, 128),), jnp.float32)
    out_weight = scatter_about(key_of[8], (NOUT, FF, D), FF ** -0.5, 0.109375, ((1, 128),), jnp.float32)
    emb_grad = draw_emb_grad(jax.random.fold_in(key_of[12], 71), 0)
    emb_moment = scatter_about(key_of[10], (V, D), 1.0, 6.0, ((0, 128),), jnp.float32)
    emb_weight = scatter_about(key_of[11], (V, D), D ** -0.5, 0.21875, ((0, 128),), jnp.float32)
    return {"sq_grad": sq_grad, "sq_moment": sq_moment, "sq_weight": sq_weight, "in_grad": in_grad, "in_moment": in_moment, "in_weight": in_weight, "out_grad": out_grad, "out_moment": out_moment, "out_weight": out_weight, "emb_grad": emb_grad, "emb_moment": emb_moment, "emb_weight": emb_weight}


FIRST_COEF = 3.4445
SECOND_COEF = -4.775
THIRD_COEF = 2.0315
MOMENTUM_DECAY = 0.95
STEP_RATE = 0.004
WEIGHT_DECAY = 0.1
EPSILON = 1e-07

def orthogonal(advance):
    row_count = advance.shape[0]
    col_count = advance.shape[1]
    frobenius = jnp.sqrt(jnp.sum(advance * advance))
    scaled = (advance / (frobenius + EPSILON)).astype(jnp.bfloat16)
    if row_count > col_count:
        scaled = scaled.T
    for sweep in range(ITERS):
        gram_matrix = jnp.dot(scaled, scaled.T, preferred_element_type=jnp.float32).astype(jnp.bfloat16)
        square = jnp.dot(gram_matrix, gram_matrix, preferred_element_type=jnp.float32)
        polynomial = (SECOND_COEF * gram_matrix.astype(jnp.float32) + THIRD_COEF * square).astype(jnp.bfloat16)
        product = jnp.dot(polynomial, scaled, preferred_element_type=jnp.float32)
        scaled = (FIRST_COEF * scaled.astype(jnp.float32) + product).astype(jnp.bfloat16)
    if row_count > col_count:
        scaled = scaled.T
    return math.sqrt(max(row_count, col_count)) * scaled.astype(jnp.float32)

def update_group(gradient, previous, weight_stack):
    moment_new = MOMENTUM_DECAY * previous + gradient
    advance = gradient + MOMENTUM_DECAY * moment_new
    direction = lax.map(orthogonal, advance)
    weight_new = weight_stack - STEP_RATE * (direction + WEIGHT_DECAY * weight_stack)
    return (moment_new, weight_new, direction)

def reference(sq_grad, sq_moment, sq_weight, in_grad, in_moment, in_weight, out_grad, out_moment, out_weight, emb_grad, emb_moment, emb_weight):
    sq_moment_new, sq_weight_new, sq_direction = update_group(sq_grad, sq_moment, sq_weight)
    in_moment_new, in_weight_new, in_direction = update_group(in_grad, in_moment, in_weight)
    out_moment_new, out_weight_new, out_direction = update_group(out_grad, out_moment, out_weight)
    emb_moment_new, emb_weight_new, emb_direction = update_group(emb_grad[None], emb_moment[None], emb_weight[None])
    return (sq_moment_new, sq_weight_new, sq_direction, in_moment_new, in_weight_new, in_direction, out_moment_new, out_weight_new, out_direction, emb_moment_new[0], emb_weight_new[0], emb_direction[0])
```

```python
import functools
import math

import jax
import jax.numpy as jnp
from jax import lax
from jax.experimental import pallas as pl
from jax.experimental.pallas import tpu as pltpu
from jax.sharding import PartitionSpec as P

A1 = 3.4445
B1 = -4.775
C1 = 2.0315
MOMENTUM_DECAY = 0.95
STEP_RATE = 0.004
WEIGHT_DECAY = 0.1
EPSILON = 1e-07
AXES = ("rep", "shard")
BF = jnp.bfloat16
F32 = jnp.float32
STEP = 256


def product(lhs, rhs, dims):
    return lax.dot_general(lhs, rhs, (dims, ((), ())), preferred_element_type=F32)


def blocks(width, body):
    def step(n, carry):
        body(pl.ds(pl.multiple_of(n * STEP, STEP), STEP))
        return carry

    lax.fori_loop(0, width // STEP, step, 0)


def gather_unit(recv, x, u, rows, src, width):
    for r in range(rows):
        k = (u * rows + r) * width
        x[u, r * src : (r + 1) * src, :] = recv[:, k : k + width]


def gram_kernel(kind, recv, own, x, *, rows, src, width):
    for wanted in (1, 2):

        @pl.when(kind[0] == wanted)
        def _():
            for u in range(2):
                gather_unit(recv, x, u, rows, src, width)

            def body(cols):
                if wanted == 1:
                    total = product(x[0], x[0, cols, :], ((1,), (1,)))
                    total += product(x[1], x[1, cols, :], ((1,), (1,)))
                else:
                    total = product(x[0], x[0, :, cols], ((0,), (0,)))
                    total += product(x[1], x[1, :, cols], ((0,), (0,)))
                own[:, cols] = total.astype(BF)

            blocks(width, body)


def chain_kernel(kind, recv, own, other, out, x, g, p, q, t, r_acc, *, rows, src, width):
    def poly(dst):
        def body(cols):
            square = product(g[...], g[:, cols], ((1,), (0,)))
            dst[:, cols] = (B1 * g[:, cols].astype(F32) + C1 * square).astype(BF)

        blocks(width, body)

    def scale_unit(u, scale):
        x[u] = (x[u].astype(F32) * scale).astype(BF)

    @pl.when(kind[0] == 0)
    def _():
        for u in range(2):
            gather_unit(recv, x, u, rows, src, width)

        def one(u, carry):
            xf = x[u].astype(F32)
            scale_unit(u, 1.0 / (jnp.sqrt(jnp.sum(xf * xf)) + EPSILON))

            def sweep(i, inner):
                def gram(cols):
                    g[:, cols] = product(x[u], x[u, cols, :], ((1,), (1,))).astype(BF)

                blocks(width, gram)
                poly(p)

                def apply(cols):
                    value = A1 * x[u, :, cols].astype(F32) + product(p[...], x[u, :, cols], ((1,), (0,)))
                    t[:, cols] = value.astype(BF)

                blocks(width, apply)
                x[u] = t[...]
                return inner

            return lax.fori_loop(0, 3, sweep, carry)

        lax.fori_loop(0, 2, one, 0)
        for u in range(2):
            for r in range(rows):
                k = (u * rows + r) * width
                out[:, k : k + width] = x[u, r * src : (r + 1) * src, :]

    @pl.when((kind[0] == 1) | (kind[0] == 2))
    def _():
        for u in range(2):
            gather_unit(recv, x, u, rows, src, width)
        total = own[...].astype(F32) + other[...].astype(F32)
        row = lax.broadcasted_iota(jnp.int32, (width, width), 0)
        col = lax.broadcasted_iota(jnp.int32, (width, width), 1)
        trace = jnp.sum(jnp.where(row == col, total, 0.0))
        scale = 1.0 / (jnp.sqrt(trace) + EPSILON)
        g[...] = ((total * scale) * scale).astype(BF)
        for u in range(2):
            scale_unit(u, scale)

        def advance_gram(poly_ref):
            def first(cols):
                t[:, cols] = (
                    A1 * g[:, cols].astype(F32) + product(poly_ref[...], g[:, cols], ((1,), (0,)))
                ).astype(BF)

            blocks(width, first)

            def second(cols):
                g[:, cols] = (
                    A1 * t[:, cols].astype(F32) + product(t[...], poly_ref[:, cols], ((1,), (0,)))
                ).astype(BF)

            blocks(width, second)

        poly(p)
        advance_gram(p)
        poly(q)

        def join(cols):
            both = p[:, cols].astype(F32) + q[:, cols].astype(F32)
            r_acc[:, cols] = (A1 * both + product(q[...], p[:, cols], ((1,), (0,)))).astype(BF)

        blocks(width, join)
        advance_gram(q)
        poly(p)

        def close(cols):
            linear = A1 * r_acc[:, cols].astype(F32) + (A1 * A1) * p[:, cols].astype(F32)
            t[:, cols] = (linear + product(p[...], r_acc[:, cols], ((1,), (0,)))).astype(BF)

        blocks(width, close)
        for wanted in (1, 2):

            @pl.when(kind[0] == wanted)
            def _():
                def apply(k, carry):
                    u, n = k // (width // STEP), k % (width // STEP)
                    cols = pl.ds(pl.multiple_of(n * STEP, STEP), STEP)
                    value = (A1 * A1 * A1) * x[u, :, cols].astype(F32)
                    if wanted == 1:
                        value += product(t[...], x[u, :, cols], ((1,), (0,)))
                    else:
                        value += product(x[u], t[:, cols], ((1,), (0,)))
                    value = value.astype(BF)
                    for r in range(rows):
                        at = pl.multiple_of((u * rows + r) * width + n * STEP, STEP)
                        out[:, pl.ds(at, STEP)] = value[r * src : (r + 1) * src]
                    return carry

                lax.fori_loop(0, 2 * (width // STEP), apply, 0)


def on_device(
    sq_grad, sq_moment, sq_weight, in_grad, in_moment, in_weight,
    out_grad, out_moment, out_weight, emb_grad, emb_moment, emb_weight,
):
    devices = lax.axis_size(AXES)
    me = lax.axis_index(AXES)
    nsq, rows, width = sq_grad.shape
    nin, _, hidden = in_grad.shape
    nout = out_grad.shape[0]
    load = 2 * rows * width
    own_sq, own_in, own_out = nsq // 2, 2 * nin, 2 * nout
    used = own_sq + own_in + own_out + 2

    def momentum(gradient, previous):
        moment = MOMENTUM_DECAY * previous + gradient
        return moment, (gradient + MOMENTUM_DECAY * moment).astype(BF)

    sq_mom, sq_adv = momentum(sq_grad, sq_moment)
    in_mom, in_adv = momentum(in_grad, in_moment)
    out_mom, out_adv = momentum(out_grad, out_moment)
    emb_mom, emb_adv = momentum(emb_grad, emb_moment)
    in_load = in_adv.reshape(nin, rows, 4, width).transpose(0, 2, 1, 3)
    outgoing = jnp.concatenate(
        [
            sq_adv.reshape(own_sq, load),
            in_load.reshape(own_in, load),
            out_adv.reshape(own_out, load),
            emb_adv.reshape(2, load),
            jnp.zeros((devices - used, load), BF),
        ]
    )
    recv = lax.all_to_all(outgoing, AXES, split_axis=0, concat_axis=0, tiled=True)
    kind = jnp.where(me < own_sq, 0, jnp.where(me < own_sq + own_in, 1, jnp.where(me < used, 2, 3)))
    kind = kind.astype(jnp.int32).reshape(1)
    sizes = dict(rows=rows, src=devices, width=width)
    vmem = pl.BlockSpec(memory_space=pltpu.VMEM)
    smem = pl.BlockSpec(memory_space=pltpu.SMEM)
    params = pltpu.CompilerParams(vmem_limit_bytes=56 << 20)
    units = pltpu.VMEM((2, width, width), BF)
    plane = pltpu.VMEM((width, width), BF)
    own = pl.pallas_call(
        functools.partial(gram_kernel, **sizes),
        out_shape=jax.ShapeDtypeStruct((width, width), BF),
        in_specs=[smem, vmem],
        out_specs=vmem,
        scratch_shapes=[units],
        compiler_params=params,
        name="gram",
    )(kind, recv)
    other = lax.ppermute(own, AXES, [(i, i ^ 1) for i in range(devices)])
    result = pl.pallas_call(
        functools.partial(chain_kernel, **sizes),
        out_shape=jax.ShapeDtypeStruct((devices, load), BF),
        in_specs=[smem, vmem, vmem, vmem],
        out_specs=vmem,
        scratch_shapes=[units, plane, plane, plane, plane, plane],
        compiler_params=params,
        name="chain",
    )(kind, recv, own, other)
    back = lax.all_to_all(result, AXES, split_axis=0, concat_axis=0, tiled=True)
    sq_found = back[:own_sq].reshape(nsq, rows, width)
    at = own_sq
    in_found = back[at : at + own_in].reshape(nin, 4, rows, width)
    in_found = in_found.transpose(0, 2, 1, 3).reshape(nin, rows, hidden)
    at += own_in
    out_found = back[at : at + own_out].reshape(nout, 4 * rows, width)
    at += own_out
    emb_found = back[at : at + 2].reshape(4 * rows, width)

    def finish(found, factor, weight):
        direction = math.sqrt(factor) * found.astype(F32)
        return weight - STEP_RATE * (direction + WEIGHT_DECAY * weight), direction

    return (
        sq_mom, *finish(sq_found, width, sq_weight),
        in_mom, *finish(in_found, hidden, in_weight),
        out_mom, *finish(out_found, hidden, out_weight),
        emb_mom, *finish(emb_found, hidden, emb_weight),
    )


def solution(mesh):
    stack = P(None, AXES, None)
    flat = P(AXES, None)
    specs = (stack,) * 9 + (flat,) * 3
    return jax.shard_map(on_device, mesh=mesh, in_specs=specs, out_specs=specs, check_vma=False)
```
